256 devices in a mesh: row: 8 (over z), col: 32 (over x, y, core).
Axes of the slice: x: 4, y: 4, z: 8, core: 2. Of those that a mesh axis runs over, the one named last changes fastest.
Arguments:
- inputs: bfloat16 [1024, 16, 1024], P('col', 'row'), may hold values from -6 to 6
- weight: bfloat16 [1024, 27, 1024], P('col', None, 'row'), may hold values from -0.0390625 to 0.0390625
- grad_out: bfloat16 [1024, 16, 1024], P('col', 'row'), may hold values from -6 to 6
Outputs:
- outputs: bfloat16 [1024, 16, 1024], P('col', 'row')
- grad_in: bfloat16 [1024, 16, 1024], P('col', 'row')
- grad_weight: float32 [1024, 27, 1024], P('col', None, 'row')
The draws below stay inside these ranges and needn't reach their ends.
All inputs are finite; a program needn't handle non-finite values.
Results may differ from the reference program's by a relative error of at most 0.0011.
Values may be sent and summed in bfloat16 or wider, within the bound.
A program may use at most 128 MiB of HBM per device.

```python
import math
import jax
import jax.numpy as jnp
from jax import lax

C = 1024
BX = 32
BY = 32
Z = 16


def block_scale(stream_key, dims, pieces, low, top_value):
    loudness = 1.0
    for axis_at, shards_of in pieces:
        draws = jax.random.uniform(jax.random.fold_in(jax.random.fold_in(stream_key, 6), axis_at), (shards_of,), jnp.float32, low / len(pieces), top_value / len(pieces))
        loudness = loudness * jnp.repeat(jnp.exp(draws), dims[axis_at] // shards_of).reshape((-1,) + (1,) * (len(dims) - 1 - axis_at))
    return loudness


def centred(key, dims, width, bound, cuts=(), kind=jnp.bfloat16):
    entries = jax.random.normal(key, dims, jnp.float32) * width
    if len(cuts) > 0:
        entries = block_scale(key, dims, cuts, -0.22, 0.18) * entries
    return jnp.clip(entries, min=-bound, max=bound).astype(kind)


def setup_inputs(seed: int = 0) -> dict:
    splits = jax.random.split(jax.random.key(seed), 4)
    inputs = centred(splits[0], (C, Z, BY * BX), 1.0, 6.0, ((0, 32), (1, 8)))
    weight = centred(splits[1], (C, 27, C), (27 * C) ** -0.5, 0.0390625, ((0, 32), (2, 8)))
    grad_out = centred(splits[2], (C, Z, BY * BX), 1.0, 6.0, ((0, 32), (1, 8)))
    return {"inputs": inputs, "weight": weight, "grad_out": grad_out}


kernel_offsets = [(a, b, e) for a in (-1, 0, 1) for b in (-1, 0, 1) for e in (-1, 0, 1)]

def plane_valid(shift_y, shift_x, extent):
    positions = jnp.arange(extent, dtype=jnp.int32) % (BY * BX)
    along_y = positions // BX + shift_y
    along_x = positions % BX + shift_x
    return (along_y >= 0) & (along_y < BY) & (along_x >= 0) & (along_x < BX)

def flat_rim(field):
    flattened = field.reshape(field.shape[0], -1)
    return jnp.pad(flattened, ((0, 0), (BX + 1, BX + 1)))

def shifted(flattened, planes, shift_z, shift_y, shift_x):
    extent = planes * BY * BX
    offset = BX + 1 + (1 + shift_z) * BY * BX + shift_y * BX + shift_x
    window = lax.slice_in_dim(flattened, offset, offset + extent, axis=1)
    return jnp.where(plane_valid(shift_y, shift_x, extent)[None, :], window, jnp.zeros_like(window))

def reference(inputs, weight, grad_out):
    channels = inputs.shape[0]
    planes = inputs.shape[1]
    extent = planes * BY * BX
    padded_in = flat_rim(jnp.pad(inputs, ((0, 0), (1, 1), (0, 0))))
    padded_grad = flat_rim(jnp.pad(grad_out, ((0, 0), (1, 1), (0, 0))))
    grad_rows = grad_out.reshape(channels, extent)
    output_sum = jnp.zeros((channels, extent), jnp.float32)
    input_sum = jnp.zeros((channels, extent), jnp.float32)
    weight_parts = []
    for k, (shift_z, shift_y, shift_x) in enumerate(kernel_offsets):
        moved = shifted(padded_in, planes, shift_z, shift_y, shift_x)
        output_sum = output_sum + jnp.dot(weight[:, k, :], moved, preferred_element_type=jnp.float32)
        moved_back = shifted(padded_grad, planes, -shift_z, -shift_y, -shift_x)
        input_sum = input_sum + jnp.dot(weight[:, k, :].T, moved_back, preferred_element_type=jnp.float32)
        weight_parts.append(jnp.dot(grad_rows, moved.T, preferred_element_type=jnp.float32))
    scale = 1.0 / math.sqrt(planes * BY * BX)
    outputs = output_sum.astype(jnp.bfloat16).reshape(inputs.shape)
    grad_in = input_sum.astype(jnp.bfloat16).reshape(inputs.shape)
    grad_weight = jnp.stack(weight_parts, axis=1) * scale
    return (outputs, grad_in, grad_weight)
```

```python
import math

import jax
import jax.numpy as jnp
from jax import lax
from jax.experimental import pallas as pl
from jax.experimental.pallas import tpu as pltpu
from jax.sharding import PartitionSpec as P

BX = 32
BY = 32
N = BX * BY
MESH = pl.DeviceIdType.MESH
f32 = jnp.float32
bf16 = jnp.bfloat16
SHIFTS = [(b, e) for b in (-1, 0, 1) for e in (-1, 0, 1)]
NX, NY, NZ = 4, 4, 8
SLICES = 4
SL = 2048 // SLICES
NMSG = 128


def valid(dy, dx):
    lane = lax.broadcasted_iota(jnp.int32, (1, N), 1)
    y = lane // BX + dy
    x = lane % BX + dx
    return (y >= 0) & (y < BY) & (x >= 0) & (x < BX)


def kernel(x_in, w_in, g_in, out_ref, gi_ref, gw_ref,
           xf, wf, wt, mg, gip, gwp, yv, halo, r0, ra, rb, rg, edge_s, edge_r, ssem, rsem):
    r = lax.axis_index("row")
    c = lax.axis_index("col")
    x, y, k = c // 8, (c // 2) % 4, c % 2
    p = x * (1 - k) + y * k
    q = y * (1 - k) + x * k
    sa, sb = 8 - 6 * k, 2 + 6 * k

    def col(pp, qq):
        return lax.rem(pp + 8, 4) * sa + lax.rem(qq + 8, 4) * sb + k

    right_a, left_a = (r, col(p + 1, q)), (r, col(p - 1, q))
    right_b, left_b = (r, col(p, q + 1)), (r, col(p, q - 1))
    up, down = (lax.rem(r + 1, NZ), c), (lax.rem(r + 7, NZ), c)
    twin = (r, c + 1 - 2 * k)

    barrier = pltpu.get_barrier_semaphore()
    for peer in (right_a, left_a, right_b, left_b, up, down, twin):
        pl.semaphore_signal(barrier, inc=1, device_id=peer, device_id_type=MESH)
    pl.semaphore_wait(barrier, 7)

    made = []

    def send(src, dst, peer):
        i = len(made)
        copy = pltpu.make_async_remote_copy(
            src_ref=src, dst_ref=dst, send_sem=ssem.at[i], recv_sem=rsem.at[i],
            device_id=peer, device_id_type=MESH)
        copy.start()
        made.append(copy)
        return copy

    def rows(base, size, unit):
        return pl.ds(pl.multiple_of(base, unit), size)

    def block(pp, qq, half=None):
        base = col(pp, qq) * 32
        if half is None:
            return xf.at[rows(base, 32, 32)]
        return xf.at[rows(base + 16 * half, 16, 16)]

    def wcols(rr):
        return rows(lax.rem(rr + 16, NZ) * 128, 128, 128)

    h_up = send(g_in.at[1], halo.at[0], up)
    h_dn = send(g_in.at[0], halo.at[1], down)
    a0 = send(x_in, block(p, q), right_a)
    a1 = send(x_in, block(p, q), left_a)
    b0 = {0: send(x_in, block(p, q), right_b)}
    b1 = {0: send(x_in, block(p, q), left_b)}
    wu = [send(w_in, wf.at[:, wcols(r)], up)]
    wd = [send(w_in, wf.at[:, wcols(r)], down)]
    tw = [send(x_in, block(p, q), twin)]
    xf[rows(c * 32, 32, 32), :] = x_in[...]
    wf[:, wcols(r)] = w_in[...]

    def build(src, plane):
        for j, (b, e) in enumerate(SHIFTS):
            s = (b * BX + e) % N
            v = src
            if s:
                v = jnp.where(valid(-b, -e), pltpu.roll(src, s, 1), 0.0)
            v = v.astype(bf16)
            for a in (-1, 0, 1):
                if plane + a in (0, 1):
                    lo = (a + 1) * 288 + j * 32
                    mg[lo:lo + 32, (plane + a) * N:(plane + a + 1) * N] = v

    def turn(rr):
        rr = lax.rem(rr + 16, NZ)
        blk = wf[:, rows(rr * 128, 128, 128)].T
        for i in range(4):
            core, dy = i % 2, i // 2
            xx, yy = rr // 2, 2 * lax.rem(rr, 2) + dy
            pos = core * 16 + (xx * 4 + yy if core == 0 else yy * 4 + xx)
            wt[rows(pos * 32, 32, 32), 0:864] = blk[i * 32:(i + 1) * 32]

    def forward_a(copy, d, back):
        copy.wait_recv()
        half = send(block(p + d, q, back), block(p + d, q, back), right_a if d < 0 else left_a)
        b0[d] = send(block(p + d, q), block(p + d, q), right_b)
        b1[d] = send(block(p + d, q), block(p + d, q), left_b)
        tw.append(send(block(p + d, q), block(p + d, q), twin))
        return half

    halves = {}

    def forward_b(d):
        b0[d].wait_recv()
        u = send(block(p + d, q - 1, 0), block(p + d, q - 1, 0), right_b)
        tw.append(send(block(p + d, q - 1), block(p + d, q - 1), twin))
        b1[d].wait_recv()
        v = send(block(p + d, q + 1, 1), block(p + d, q + 1, 1), left_b)
        tw.append(send(block(p + d, q + 1), block(p + d, q + 1), twin))
        halves[d] = (u, v)

    def finish_b(d):
        halves[d][0].wait_recv()
        halves[d][1].wait_recv()
        tw.append(send(block(p + d, q + 2), block(p + d, q + 2), twin))

    def forward_w(step):
        wu[-1].wait_recv()
        wd[-1].wait_recv()
        lo, hi = wcols(r - step), wcols(r + step)
        if step < 3:
            wu.append(send(wf.at[:, lo], wf.at[:, lo], up))
            wd.append(send(wf.at[:, hi], wf.at[:, hi], down))
        else:
            wu.append(send(wf.at[0:432, lo], wf.at[0:432, lo], up))
            wd.append(send(wf.at[432:864, hi], wf.at[432:864, hi], down))

    a2 = forward_a(a0, -1, 0)
    a3 = forward_a(a1, 1, 1)
    build(g_in[0].astype(f32), 0)
    forward_b(0)
    a2.wait_recv()
    a3.wait_recv()
    b0[2] = send(block(p + 2, q), block(p + 2, q), right_b)
    b1[2] = send(block(p + 2, q), block(p + 2, q), left_b)
    tw.append(send(block(p + 2, q), block(p + 2, q), twin))
    build(g_in[1].astype(f32), 1)
    forward_b(-1)
    forward_w(1)
    forward_b(1)
    finish_b(0)
    h_up.wait_recv()
    build(jnp.where(r == 0, 0.0, halo[0].astype(f32)), -1)
    finish_b(-1)
    forward_b(2)
    h_dn.wait_recv()
    build(jnp.where(r == NZ - 1, 0.0, halo[1].astype(f32)), 2)
    finish_b(1)
    finish_b(2)
    turn(r)
    turn(r - 1)
    turn(r + 1)
    forward_w(2)
    for copy in tw:
        copy.wait_recv()

    def gw_tile(i, carry):
        lo = rows(i * 256, 256, 256)
        for m in range(2):
            gwp[m * 432:(m + 1) * 432, lo] = lax.dot_general(
                mg[m * 432:(m + 1) * 432, :], xf[lo, :], (((1,), (1,)), ((), ())),
                preferred_element_type=f32)
        return carry

    lax.fori_loop(0, 2, gw_tile, 0)
    forward_w(3)
    lax.fori_loop(2, 4, gw_tile, 0)

    top, bot = (0, 432), (432, 432)

    def gpart(d, half):
        return (pl.ds(*half), wcols(r + d))

    sent_u, sent_d = [], []

    def gw_send(direction, d, half):
        sent = sent_u if direction > 0 else sent_d
        slot = rg.at[0 if direction > 0 else 1, len(sent)]
        sent.append(send(gwp.at[gpart(d, half)], slot, up if direction > 0 else down))

    def gw_step(i):
        for direction, sent in ((1, sent_u), (-1, sent_d)):
            first, second = (top, bot) if direction > 0 else (bot, top)
            half = first if i % 2 == 0 else second
            d = direction * (3 - (i + 1) // 2)
            sent[i].wait_recv()
            at = gpart(d, half)
            gwp[at] = gwp[at] + rg[0 if direction > 0 else 1, i]
            if d != 0:
                gw_send(direction, d, half)

    gw_send(1, 4, top)
    gw_send(-1, -4, bot)
    gw_send(1, 3, bot)
    gw_send(-1, -3, top)

    for d in (-2, 2, -3, 3):
        turn(r + d)
    wu[-1].wait_recv()
    wd[-1].wait_recv()
    turn(r + 4)

    mine, other = k * 512, (1 - k) * 512

    def gi_slice(l):
        for t in range(SL // 256):
            lo = l * SL + t * 256
            for m in range(2):
                gip[m * 512:(m + 1) * 512, lo:lo + 256] = jnp.dot(
                    wt[m * 512:(m + 1) * 512, 0:864], mg[:, lo:lo + 256], preferred_element_type=f32)
        at = pl.ds(l * SL, SL)
        return send(gip.at[rows(other, 512, 512), at], r0.at[:, at], twin)

    def pass_one(l, base, unit, pos, right, left, buf):
        half = unit // 2
        at = pl.ds(l * SL, SL)

        def part(d, which):
            return (rows(base + lax.rem(pos + d + 8, 4) * unit + which * half, half, half), at)

        def go(i, d, which, peer):
            return send(gip.at[part(d, which)], buf.at[i, :, at], peer)

        first = [go(0, 2, 0, right), go(1, 2, 1, left), go(2, 1, 1, right), go(3, -1, 0, left)]

        def second():
            first[0].wait_recv()
            here = part(1, 0)
            gip[here] = gip[here] + buf[0, :, at]
            first.append(go(4, 1, 0, right))
            first[1].wait_recv()
            here = part(-1, 1)
            gip[here] = gip[here] + buf[1, :, at]
            first.append(go(5, -1, 1, left))

        def third():
            first[2].wait_recv()
            first[5].wait_recv()
            here = part(0, 1)
            gip[here] = gip[here] + (buf[2, :, at] + buf[5, :, at])
            first[3].wait_recv()
            first[4].wait_recv()
            here = part(0, 0)
            gip[here] = gip[here] + (buf[3, :, at] + buf[4, :, at])

        return second, third

    pair, stage_a, stage_b = {}, {}, {}

    def join(l):
        pair[l].wait_recv()
        here = (rows(mine, 512, 512), pl.ds(l * SL, SL))
        gip[here] = gip[here] + r0[:, pl.ds(l * SL, SL)]
        stage_a[l] = pass_one(l, mine, 128, p, right_a, left_a, ra)

    def step_b(l):
        stage_a[l][1]()
        stage_b[l] = pass_one(l, mine + p * 128, 32, q, right_b, left_b, rb)

    pair[0] = gi_slice(0)
    pair[1] = gi_slice(1)
    join(0)
    gw_step(0)
    pair[2] = gi_slice(2)
    join(1)
    stage_a[0][0]()
    pair[3] = gi_slice(3)
    join(2)
    gw_step(1)
    stage_a[1][0]()
    join(3)
    step_b(0)

    def y_tile(n, carry):
        lo = rows(n * 256, 256, 256)
        for m in range(2):
            yv[m * 432:(m + 1) * 432, lo] = jnp.dot(
                wf[m * 432:(m + 1) * 432, :], xf[:, lo], preferred_element_type=f32)
        return carry

    lax.fori_loop(0, 4, y_tile, 0)
    gw_step(2)
    stage_a[2][0]()
    step_b(1)
    stage_b[0][0]()
    lax.fori_loop(4, 8, y_tile, 0)
    stage_a[3][0]()
    gw_step(3)

    def plane(z):
        acc = None
        for j, (b, e) in enumerate(SHIFTS):
            t = None
            for a in (-1, 0, 1):
                if z + a in (0, 1):
                    lo = (a + 1) * 288 + j * 32
                    u = yv[lo:lo + 32, (z + a) * N:(z + a + 1) * N]
                    t = u if t is None else t + u
            s = (-(b * BX + e)) % N
            if s:
                t = jnp.where(valid(b, e), pltpu.roll(t, s, 1), 0.0)
            acc = t if acc is None else acc + t
        return acc

    edge_s[0] = plane(-1)
    e_dn = send(edge_s.at[0], edge_r.at[0], down)
    edge_s[1] = plane(2)
    e_up = send(edge_s.at[1], edge_r.at[1], up)
    step_b(2)
    stage_b[1][0]()
    gw_step(4)
    own0 = plane(0)
    own1 = plane(1)
    step_b(3)
    stage_b[0][1]()
    stage_b[2][0]()
    e_up.wait_recv()
    out_ref[0] = (own0 + jnp.where(r == 0, 0.0, edge_r[1])).astype(bf16)
    e_dn.wait_recv()
    out_ref[1] = (own1 + jnp.where(r == NZ - 1, 0.0, edge_r[0])).astype(bf16)
    stage_b[1][1]()
    stage_b[3][0]()
    stage_b[2][1]()
    stage_b[3][1]()
    gi_ref[...] = gip[rows(mine + p * 128 + q * 32, 32, 32), :].astype(bf16)
    gw_step(5)
    gw_step(6)
    gw_ref[...] = gwp[:, wcols(r)] * (1.0 / math.sqrt(16 * N))
    for copy in made:
        copy.wait_send()


def on_device(inputs, weight, grad_out):
    xr = inputs.reshape(32, 2 * N)
    wr = weight.transpose(1, 0, 2).reshape(27 * 32, 128)
    gr = grad_out.transpose(1, 0, 2)
    vm = pl.BlockSpec(memory_space=pltpu.VMEM)
    out, gi, gw = pl.pallas_call(
        kernel,
        out_shape=(jax.ShapeDtypeStruct((2, 32, N), bf16),
                   jax.ShapeDtypeStruct((32, 2 * N), bf16),
                   jax.ShapeDtypeStruct((864, 128), f32)),
        in_specs=[vm] * 3,
        out_specs=(vm,) * 3,
        scratch_shapes=[
            pltpu.VMEM((1024, 2 * N), bf16),
            pltpu.VMEM((864, 1024), bf16),
            pltpu.VMEM((1024, 896), bf16),
            pltpu.VMEM((864, 2 * N), bf16),
            pltpu.VMEM((1024, 2 * N), f32),
            pltpu.VMEM((864, 1024), f32),
            pltpu.VMEM((864, 2 * N), f32),
            pltpu.VMEM((2, 32, N), bf16),
            pltpu.VMEM((512, 2 * N), f32),
            pltpu.VMEM((6, 64, 2 * N), f32),
            pltpu.VMEM((6, 16, 2 * N), f32),
            pltpu.VMEM((2, 7, 432, 128), f32),
            pltpu.VMEM((2, 32, N), f32),
            pltpu.VMEM((2, 32, N), f32),
            pltpu.SemaphoreType.DMA((NMSG,)),
            pltpu.SemaphoreType.DMA((NMSG,)),
        ],
        compiler_params=pltpu.CompilerParams(
            collective_id=0, has_side_effects=True, vmem_limit_bytes=58 << 20),
        name="layer",
    )(xr, wr, gr)
    return (out.transpose(1, 0, 2), gi.reshape(32, 2, N),
            gw.reshape(27, 32, 128).transpose(1, 0, 2))


def solution(mesh):
    placed = (P("col", "row", None), P("col", None, "row"), P("col", "row", None))
    return jax.shard_map(on_device, mesh=mesh, in_specs=placed, out_specs=placed[:1] * 2 + placed[1:2], check_vma=False)
```

```python
import math

import jax
import jax.numpy as jnp
from jax import lax
from jax.experimental import pallas as pl
from jax.experimental.pallas import tpu as pltpu
from jax.sharding import PartitionSpec as P

BX = 32
BY = 32
N = BX * BY
MESH = pl.DeviceIdType.MESH
f32 = jnp.float32
bf16 = jnp.bfloat16
SHIFTS = [(b, e) for b in (-1, 0, 1) for e in (-1, 0, 1)]
NX, NY, NZ = 4, 4, 8
SLICES = 4
SL = 2048 // SLICES
NMSG = 208
SCHED = (
    "s0", "t1", "s1", "s2", "j0", "g0", "t2", "y0", "s3", "j1", "a0", "g1", "y1", "y2",
    "t3", "j2", "a1", "b0", "g2", "y3", "y4", "y5", "j3", "a2", "b1", "c0", "g3", "y6",
    "y7", "p-1", "a3", "b2", "c1", "f0", "g4", "p2", "b3", "c2", "f1", "p0", "c3", "f2",
    "g5", "p1", "f3", "o0", "o1", "g6",
)


def valid(dy, dx):
    lane = lax.broadcasted_iota(jnp.int32, (1, N), 1)
    y = lane // BX + dy
    x = lane % BX + dx
    return (y >= 0) & (y < BY) & (x >= 0) & (x < BX)


def kernel(x_in, w_in, g_in, out_ref, gi_ref, gw_ref,
           xf, wf, wt, mg, gip, gwp, yv, halo, r0, ra, rb, rg, sg, edge_s, edge_r, ssem, rsem):
    r = lax.axis_index("row")
    c = lax.axis_index("col")
    x, y, k = c // 8, (c // 2) % 4, c % 2
    p = x * (1 - k) + y * k
    q = y * (1 - k) + x * k
    sa, sb = 8 - 6 * k, 2 + 6 * k

    def col(pp, qq):
        return lax.rem(pp + 8, 4) * sa + lax.rem(qq + 8, 4) * sb + k

    right_a, left_a = (r, col(p + 1, q)), (r, col(p - 1, q))
    right_b, left_b = (r, col(p, q + 1)), (r, col(p, q - 1))
    up, down = (lax.rem(r + 1, NZ), c), (lax.rem(r + 7, NZ), c)
    twin = (r, c + 1 - 2 * k)

    barrier = pltpu.get_barrier_semaphore()
    for peer in (right_a, left_a, right_b, left_b, up, down, twin):
        pl.semaphore_signal(barrier, inc=1, device_id=peer, device_id_type=MESH)
    pl.semaphore_wait(barrier, 7)

    made = []

    def send(src, dst, peer):
        i = len(made)
        copy = pltpu.make_async_remote_copy(
            src_ref=src, dst_ref=dst, send_sem=ssem.at[i], recv_sem=rsem.at[i],
            device_id=peer, device_id_type=MESH)
        copy.start()
        made.append(copy)
        return copy

    def rows(base, size, unit):
        return pl.ds(pl.multiple_of(base, unit), size)

    def block(pp, qq):
        return xf.at[rows(col(pp, qq) * 32, 32, 32)]

    def unit(pp, qq, h):
        return xf.at[rows(col(pp, qq) * 32 + 16 * h, 16, 16)]

    def wcols(rr):
        return rows(lax.rem(rr + 16, NZ) * 128, 128, 128)

    ar, al, fa = {}, {}, {}
    br, bl, fb = {}, {}, {}
    tw = []
    h_up = send(g_in.at[1], halo.at[0], up)
    h_dn = send(g_in.at[0], halo.at[1], down)
    for h in (0, 1):
        src = x_in.at[16 * h:16 * h + 16]
        other_src = x_in.at[16 - 16 * h:32 - 16 * h]
        ar[h] = send(src, unit(p, q, h), right_a)
        al[1 - h] = send(other_src, unit(p, q, 1 - h), left_a)
        br[0, h] = send(src, unit(p, q, h), right_b)
        bl[0, 1 - h] = send(other_src, unit(p, q, 1 - h), left_b)
    wu, wd = {}, {}
    for i in (0, 1):
        for step, got, peer in ((i, wu, up), (1 - i, wd, down)):
            got[0, step] = send(w_in.at[432 * step:432 * step + 432],
                                wf.at[432 * step:432 * step + 432, wcols(r)], peer)
    tw.append(send(x_in, block(p, q), twin))
    xf[rows(c * 32, 32, 32), :] = x_in[...]
    wf[:, wcols(r)] = w_in[...]

    def build(src, plane):
        for j, (b, e) in enumerate(SHIFTS):
            s = (b * BX + e) % N
            v = src
            if s:
                v = jnp.where(valid(-b, -e), pltpu.roll(src, s, 1), 0.0)
            v = v.astype(bf16)
            for a in (-1, 0, 1):
                if plane + a in (0, 1):
                    lo = (a + 1) * 288 + j * 32
                    mg[lo:lo + 32, (plane + a) * N:(plane + a + 1) * N] = v

    def gi_turn(j):
        blk = wf[:, rows(lax.rem(j + 8, 4) * 256, 256, 256)].T
        for i in range(8):
            to = (i % 2) * 128 + (i // 2) * 32
            wt[to:to + 32, 0:864] = blk[i * 32:(i + 1) * 32]

    def gi_pair(j, start, tiles):
        jj = lax.rem(j + 8, 4)

        def tile(n, carry):
            o = jnp.dot(wt[:, 0:864], mg[:, rows(n * SL, SL, SL)], preferred_element_type=f32)
            gip[n, rows(jj * 128, 128, 128), :] = o[0:128]
            for i in range(4):
                gip[n, rows(512 + i * 128 + jj * 32, 32, 32), :] = o[128 + i * 32:160 + i * 32]
            return carry

        lax.fori_loop(start, start + tiles, tile, 0)

    half_r = r // 2
    sign = 1 - 2 * lax.rem(r, 2)

    def spread_b(d, h):
        u = unit(p + d, q, h)
        if h == 0:
            br[d, h] = send(u, u, right_b)
            bl[d, h] = send(u, u, left_b)
        else:
            bl[d, h] = send(u, u, left_b)
            br[d, h] = send(u, u, right_b)

    def share(pp, qq):
        tw.append(send(block(pp, qq), block(pp, qq), twin))

    def take_a(d, h):
        (ar if d < 0 else al)[h].wait_recv()
        u = unit(p + d, q, h)
        if (d, h) == (-1, 0):
            fa[0] = send(u, u, right_a)
        if (d, h) == (1, 1):
            fa[1] = send(u, u, left_a)
        spread_b(d, h)

    def take_b(d):
        br[d, 0].wait_recv()
        u = unit(p + d, q - 1, 0)
        fb[d, 0] = send(u, u, right_b)
        bl[d, 1].wait_recv()
        u = unit(p + d, q + 1, 1)
        fb[d, 1] = send(u, u, left_b)

    def rest_b(d):
        br[d, 1].wait_recv()
        share(p + d, q - 1)
        bl[d, 0].wait_recv()
        share(p + d, q + 1)

    def finish_b(d):
        fb[d, 0].wait_recv()
        fb[d, 1].wait_recv()
        share(p + d, q + 2)

    def forward_w(step, i):
        for got, peer, part, d in ((wu, up, i, -step), (wd, down, 1 - i, step)):
            got[step - 1, part].wait_recv()
            if step < 3 or (step == 3 and i == 0):
                here = wf.at[432 * part:432 * part + 432, wcols(r + d)]
                got[step, part] = send(here, here, peer)

    build(g_in[0].astype(f32), 0)
    take_a(-1, 0)
    take_a(1, 1)
    take_b(0)
    forward_w(1, 0)
    take_a(-1, 1)
    share(p - 1, q)
    take_a(1, 0)
    share(p + 1, q)
    for h in (0, 1):
        fa[h].wait_recv()
        spread_b(2, h)
    share(p + 2, q)
    rest_b(0)
    build(g_in[1].astype(f32), 1)
    take_b(-1)
    take_b(1)
    forward_w(1, 1)
    h_up.wait_recv()
    build(jnp.where(r == 0, 0.0, halo[0].astype(f32)), -1)
    finish_b(0)
    rest_b(-1)
    rest_b(1)
    forward_w(2, 0)
    h_dn.wait_recv()
    build(jnp.where(r == NZ - 1, 0.0, halo[1].astype(f32)), 2)
    take_b(2)
    gi_turn(half_r)
    forward_w(2, 1)
    finish_b(-1)
    finish_b(1)
    rest_b(2)
    gi_pair(half_r, 0, 2)
    forward_w(3, 0)
    gi_pair(half_r, 2, 2)
    finish_b(2)
    gi_turn(half_r - sign)
    gi_pair(half_r - sign, 0, 2)
    forward_w(3, 1)
    gi_pair(half_r - sign, 2, 2)
    gi_turn(half_r + sign)
    for copy in tw:
        copy.wait_recv()

    def gw_tile(j):
        lo = rows(lax.rem(j + 8, 4) * 256, 256, 256)

        def part(m, carry):
            at = rows(m * 432, 432, 16)
            gwp[at, lo] = lax.dot_general(
                mg[at, :], xf[lo, :], (((1,), (1,)), ((), ())), preferred_element_type=f32)
            return carry

        lax.fori_loop(0, 2, part, 0)

    top, bot = (0, 448), (448, 416)

    def gpart(d, half):
        return (pl.ds(*half), wcols(r + d))

    def pack(v, dst):
        n = v.shape[0]
        hi = v.astype(bf16)
        h = hi.astype(f32)
        big = jnp.abs(h) > 1e-34
        t = jnp.where(big, (v - h) / jnp.where(big, h, 1.0), 0.0)
        lev = jnp.floor(t * 2560.0 + 0.5)
        dst[0:n] = hi
        dst[n:n + n // 2] = (lev[:n // 2] * 21.0 + lev[n // 2:]).astype(bf16)

    def unpack(src, n):
        h = src[0:n].astype(f32)
        both = src[n:n + n // 2].astype(f32)
        first = jnp.floor((both + 10.5) * (1.0 / 21.0))
        lev = jnp.concatenate([first, both - 21.0 * first], axis=0)
        return h + h * (lev * (1.0 / 2560.0))

    sent_u, sent_d = [], []

    def gw_send(direction, d, half, v=None):
        sent = sent_u if direction > 0 else sent_d
        side, i, n = (1 - direction) // 2, len(sent), half[1]
        pack(gwp[gpart(d, half)] if v is None else v, sg.at[side, i])
        sent.append(send(sg.at[side, i, 0:n + n // 2], rg.at[side, i, 0:n + n // 2],
                         up if direction > 0 else down))

    def gw_step(i):
        for direction, sent in ((1, sent_u), (-1, sent_d)):
            first, second = (top, bot) if direction > 0 else (bot, top)
            half = first if i % 2 == 0 else second
            d = direction * (3 - (i + 1) // 2)
            sent[i].wait_recv()
            at = gpart(d, half)
            v = gwp[at] + unpack(rg.at[(1 - direction) // 2, i], half[1])
            if d != 0:
                gw_send(direction, d, half, v)
            else:
                gwp[at] = v

    gw_tile(half_r + 2)
    gw_send(1, 4, top)
    gw_send(-1, -4, bot)
    gi_pair(half_r + sign, 0, 4)
    forward_w(4, 0)
    gi_turn(half_r + 2)

    mine, other = k * 512, (1 - k) * 512

    def gi_slice(l):
        gi_pair(half_r + 2, l, 1)
        return send(gip.at[l, rows(other, 512, 512)], r0.at[l], twin)

    def pass_one(l, base, unit, pos, right, left, buf):
        half = unit // 2

        def part(d, which):
            return (l, rows(base + lax.rem(pos + d + 8, 4) * unit + which * half, half, half))

        def go(i, d, which, peer):
            return send(gip.at[part(d, which)], buf.at[l, i], peer)

        first = [go(0, 2, 0, right), go(1, 2, 1, left), go(2, 1, 1, right), go(3, -1, 0, left)]

        def second():
            first[0].wait_recv()
            here = part(1, 0)
            gip[here] = gip[here] + buf[l, 0]
            first.append(go(4, 1, 0, right))
            first[1].wait_recv()
            here = part(-1, 1)
            gip[here] = gip[here] + buf[l, 1]
            first.append(go(5, -1, 1, left))

        def third():
            first[2].wait_recv()
            first[5].wait_recv()
            here = part(0, 1)
            gip[here] = gip[here] + (buf[l, 2] + buf[l, 5])
            first[3].wait_recv()
            first[4].wait_recv()
            here = part(0, 0)
            gip[here] = gip[here] + (buf[l, 3] + buf[l, 4])

        return second, third

    pair, stage_a, stage_b = {}, {}, {}

    def join(l):
        pair[l].wait_recv()
        here = (l, rows(mine, 512, 512))
        gip[here] = gip[here] + r0[l]
        stage_a[l] = pass_one(l, mine, 128, p, right_a, left_a, ra)

    def step_b(l):
        stage_a[l][1]()
        stage_b[l] = pass_one(l, mine + p * 128, 32, q, right_b, left_b, rb)

    def y_tile(n, carry):
        lo = rows(n * 256, 256, 256)
        for m in range(2):
            yv[m * 432:(m + 1) * 432, lo] = jnp.dot(
                wf[m * 432:(m + 1) * 432, :], xf[:, lo], preferred_element_type=f32)
        return carry


    def ys(lo, hi):
        lax.fori_loop(lo, hi, y_tile, 0)

    def plane(z):
        acc = None
        for j, (b, e) in enumerate(SHIFTS):
            t = None
            for a in (-1, 0, 1):
                if z + a in (0, 1):
                    lo = (a + 1) * 288 + j * 32
                    u = yv[lo:lo + 32, (z + a) * N:(z + a + 1) * N]
                    t = u if t is None else t + u
            s = (-(b * BX + e)) % N
            if s:
                t = jnp.where(valid(b, e), pltpu.roll(t, s, 1), 0.0)
            acc = t if acc is None else acc + t
        return acc

    def step_a2(l):
        stage_a[l][0]()

    def step_b2(l):
        stage_b[l][0]()

    def finish(l):
        stage_b[l][1]()

    own, edges = {}, {}

    def step_s(l):
        pair[l] = gi_slice(l)

    def step_t(i):
        gw_tile(half_r + 2 + (0, -sign, sign, 2)[i])
        if i == 1:
            gw_send(1, 3, bot)
            gw_send(-1, -3, top)

    def step_y(n):
        ys(n, n + 1)

    def step_p(z):
        if z in (0, 1):
            own[z] = plane(z)
        else:
            i = (z + 1) // 3
            edge_s[i] = plane(z)
            edges[i] = send(edge_s.at[i], edge_r.at[i], up if i else down)

    def step_o(z):
        edges[1 - z].wait_recv()
        gone = r == (NZ - 1 if z else 0)
        out_ref[z] = (own[z] + jnp.where(gone, 0.0, edge_r[1 - z])).astype(bf16)

    ops = dict(s=step_s, t=step_t, y=step_y, p=step_p, o=step_o, g=gw_step, j=join,
               a=step_a2, b=step_b, c=step_b2, f=finish)
    for word in SCHED:
        ops[word[0]](int(word[1:]))
    for l in range(SLICES):
        gi_ref[:, l * SL:(l + 1) * SL] = gip[l, rows(mine + p * 128 + q * 32, 32, 32), :].astype(bf16)
    gw_ref[...] = gwp[:, wcols(r)] * (1.0 / math.sqrt(16 * N))
    for copy in made:
        copy.wait_send()


def on_device(inputs, weight, grad_out):
    xr = inputs.reshape(32, 2 * N)
    wr = weight.transpose(1, 0, 2).reshape(27 * 32, 128)
    gr = grad_out.transpose(1, 0, 2)
    vm = pl.BlockSpec(memory_space=pltpu.VMEM)
    out, gi, gw = pl.pallas_call(
        kernel,
        out_shape=(jax.ShapeDtypeStruct((2, 32, N), bf16),
                   jax.ShapeDtypeStruct((32, 2 * N), bf16),
                   jax.ShapeDtypeStruct((864, 128), f32)),
        in_specs=[vm] * 3,
        out_specs=(vm,) * 3,
        scratch_shapes=[
            pltpu.VMEM((1024, 2 * N), bf16),
            pltpu.VMEM((864, 1024), bf16),
            pltpu.VMEM((256, 896), bf16),
            pltpu.VMEM((864, 2 * N), bf16),
            pltpu.VMEM((SLICES, 1024, SL), f32),
            pltpu.VMEM((864, 1024), f32),
            pltpu.VMEM((864, 2 * N), f32),
            pltpu.VMEM((2, 32, N), bf16),
            pltpu.VMEM((SLICES, 512, SL), f32),
            pltpu.VMEM((SLICES, 6, 64, SL), f32),
            pltpu.VMEM((SLICES, 6, 16, SL), f32),
            pltpu.VMEM((2, 7, 672, 128), bf16),
            pltpu.VMEM((2, 7, 672, 128), bf16),
            pltpu.VMEM((2, 32, N), f32),
            pltpu.VMEM((2, 32, N), f32),
            pltpu.SemaphoreType.DMA((NMSG,)),
            pltpu.SemaphoreType.DMA((NMSG,)),
        ],
        compiler_params=pltpu.CompilerParams(
            collective_id=0, has_side_effects=True, vmem_limit_bytes=58 << 20),
        name="layer",
    )(xr, wr, gr)
    return (out.transpose(1, 0, 2), gi.reshape(32, 2, N),
            gw.reshape(27, 32, 128).transpose(1, 0, 2))


def solution(mesh):
    placed = (P("col", "row", None), P("col", None, "row"), P("col", "row", None))
    return jax.shard_map(on_device, mesh=mesh, in_specs=placed, out_specs=placed[:1] * 2 + placed[1:2], check_vma=False)
```

```python
import math

import jax
import jax.numpy as jnp
from jax import lax
from jax.experimental import pallas as pl
from jax.experimental.pallas import tpu as pltpu
from jax.sharding import PartitionSpec as P

BX = 32
BY = 32
N = BX * BY
MESH = pl.DeviceIdType.MESH
f32 = jnp.float32
bf16 = jnp.bfloat16
SHIFTS = [(b, e) for b in (-1, 0, 1) for e in (-1, 0, 1)]
NX, NY, NZ = 4, 4, 8
SLICES = 4
SL = 2048 // SLICES
NMSG = 208
SCHED = (
    "s0", "s1", "s2", "g0", "j0", "t2", "s3", "j1", "g1", "a0", "y0", "t3", "j2", "a1",
    "b0", "g2", "y1", "y2", "j3", "a2", "b1", "c0", "g3", "y3", "p-1", "a3", "b2", "c1",
    "f0", "g4", "p2", "b3", "c2", "f1", "p0", "c3", "f2", "g5", "p1", "f3", "o0", "o1",
    "g6",
)


def valid(dy, dx):
    lane = lax.broadcasted_iota(jnp.int32, (1, N), 1)
    y = lane // BX + dy
    x = lane % BX + dx
    return (y >= 0) & (y < BY) & (x >= 0) & (x < BX)


def kernel(x_in, w_in, g_in, out_ref, gi_ref, gw_ref,
           xf, wf, wt, mg, gip, gwp, yv, halo, r0, ra, rb, rg, sg, edge_s, edge_r, ssem, rsem):
    r = lax.axis_index("row")
    c = lax.axis_index("col")
    x, y, k = c // 8, (c // 2) % 4, c % 2
    p = x * (1 - k) + y * k
    q = y * (1 - k) + x * k
    sa, sb = 8 - 6 * k, 2 + 6 * k

    def col(pp, qq):
        return lax.rem(pp + 8, 4) * sa + lax.rem(qq + 8, 4) * sb + k

    right_a, left_a = (r, col(p + 1, q)), (r, col(p - 1, q))
    right_b, left_b = (r, col(p, q + 1)), (r, col(p, q - 1))
    up, down = (lax.rem(r + 1, NZ), c), (lax.rem(r + 7, NZ), c)
    twin = (r, c + 1 - 2 * k)

    barrier = pltpu.get_barrier_semaphore()
    for peer in (right_a, left_a, right_b, left_b, up, down, twin):
        pl.semaphore_signal(barrier, inc=1, device_id=peer, device_id_type=MESH)
    pl.semaphore_wait(barrier, 7)

    made = []

    def send(src, dst, peer):
        i = len(made)
        copy = pltpu.make_async_remote_copy(
            src_ref=src, dst_ref=dst, send_sem=ssem.at[i], recv_sem=rsem.at[i],
            device_id=peer, device_id_type=MESH)
        copy.start()
        made.append(copy)
        return copy

    def rows(base, size, unit):
        return pl.ds(pl.multiple_of(base, unit), size)

    def block(pp, qq):
        return xf.at[rows(col(pp, qq) * 32, 32, 32)]

    def unit(pp, qq, h):
        return xf.at[rows(col(pp, qq) * 32 + 16 * h, 16, 16)]

    def wcols(rr):
        return rows(lax.rem(rr + 16, NZ) * 128, 128, 128)

    ar, al, fa = {}, {}, {}
    br, bl, fb = {}, {}, {}
    tw = []
    h_up = send(g_in.at[1], halo.at[0], up)
    h_dn = send(g_in.at[0], halo.at[1], down)
    for z in (0, 1):
        xf[rows(c * 32, 32, 32), z * N:(z + 1) * N] = x_in[z]
    for h in (0, 1):
        src, other_src = unit(p, q, h), unit(p, q, 1 - h)
        ar[h] = send(src, src, right_a)
        al[1 - h] = send(other_src, other_src, left_a)
        br[0, h] = send(src, src, right_b)
        bl[0, 1 - h] = send(other_src, other_src, left_b)
    wu, wd = {}, {}
    for i in (0, 1):
        for step, got, peer in ((i, wu, up), (1 - i, wd, down)):
            got[0, step] = send(w_in.at[432 * step:432 * step + 432],
                                wf.at[432 * step:432 * step + 432, wcols(r)], peer)
    tw.append(send(block(p, q), block(p, q), twin))
    wf[:, wcols(r)] = w_in[...]

    def build(src, plane):
        for j, (b, e) in enumerate(SHIFTS):
            s = (b * BX + e) % N
            v = src
            if s:
                v = jnp.where(valid(-b, -e), pltpu.roll(src, s, 1), 0.0)
            v = v.astype(bf16)
            for a in (-1, 0, 1):
                if plane + a in (0, 1):
                    lo = (a + 1) * 288 + j * 32
                    mg[lo:lo + 32, (plane + a) * N:(plane + a + 1) * N] = v

    def gi_turn(j):
        blk = wf[:, rows(lax.rem(j + 8, 4) * 256, 256, 256)].T
        for i in range(8):
            to = (i % 2) * 128 + (i // 2) * 32
            wt[to:to + 32, 0:864] = blk[i * 32:(i + 1) * 32]

    def gi_pair(j, start, tiles):
        jj = lax.rem(j + 8, 4)

        def tile(n, carry):
            o = jnp.dot(wt[:, 0:864], mg[:, rows(n * SL, SL, SL)], preferred_element_type=f32)
            gip[n, rows(jj * 128, 128, 128), :] = o[0:128]
            for i in range(4):
                gip[n, rows(512 + i * 128 + jj * 32, 32, 32), :] = o[128 + i * 32:160 + i * 32]
            return carry

        lax.fori_loop(start, start + tiles, tile, 0)

    half_r = r // 2
    sign = 1 - 2 * lax.rem(r, 2)

    def spread_b(d, h):
        u = unit(p + d, q, h)
        if h == 0:
            br[d, h] = send(u, u, right_b)
            bl[d, h] = send(u, u, left_b)
        else:
            bl[d, h] = send(u, u, left_b)
            br[d, h] = send(u, u, right_b)

    def share(pp, qq):
        tw.append(send(block(pp, qq), block(pp, qq), twin))

    def take_a(d, h):
        (ar if d < 0 else al)[h].wait_recv()
        u = unit(p + d, q, h)
        if (d, h) == (-1, 0):
            fa[0] = send(u, u, right_a)
        if (d, h) == (1, 1):
            fa[1] = send(u, u, left_a)
        spread_b(d, h)

    def take_b(d):
        br[d, 0].wait_recv()
        u = unit(p + d, q - 1, 0)
        fb[d, 0] = send(u, u, right_b)
        bl[d, 1].wait_recv()
        u = unit(p + d, q + 1, 1)
        fb[d, 1] = send(u, u, left_b)

    def rest_b(d):
        br[d, 1].wait_recv()
        share(p + d, q - 1)
        bl[d, 0].wait_recv()
        share(p + d, q + 1)

    def finish_b(d):
        fb[d, 0].wait_recv()
        fb[d, 1].wait_recv()
        share(p + d, q + 2)

    def forward_w(step, i):
        for got, peer, part, d in ((wu, up, i, -step), (wd, down, 1 - i, step)):
            got[step - 1, part].wait_recv()
            if step < 3 or (step == 3 and i == 0):
                here = wf.at[432 * part:432 * part + 432, wcols(r + d)]
                got[step, part] = send(here, here, peer)

    build(g_in[0].astype(f32), 0)
    take_a(-1, 0)
    take_a(1, 1)
    take_b(0)
    forward_w(1, 0)
    take_a(-1, 1)
    share(p - 1, q)
    take_a(1, 0)
    share(p + 1, q)
    for h in (0, 1):
        fa[h].wait_recv()
        spread_b(2, h)
    share(p + 2, q)
    rest_b(0)
    build(g_in[1].astype(f32), 1)
    take_b(-1)
    take_b(1)
    forward_w(1, 1)
    h_up.wait_recv()
    build(jnp.where(r == 0, 0.0, halo[0].astype(f32)), -1)
    finish_b(0)
    rest_b(-1)
    rest_b(1)
    forward_w(2, 0)
    h_dn.wait_recv()
    build(jnp.where(r == NZ - 1, 0.0, halo[1].astype(f32)), 2)
    take_b(2)
    gi_turn(half_r)
    forward_w(2, 1)
    finish_b(-1)
    finish_b(1)
    rest_b(2)
    gi_pair(half_r, 0, 2)
    forward_w(3, 0)
    finish_b(2)
    gi_pair(half_r, 2, 2)
    for copy in tw:
        copy.wait_recv()

    def gw_tile(j):
        lo = rows(lax.rem(j + 8, 4) * 256, 256, 256)

        def part(m, carry):
            at = rows(m * 432, 432, 16)
            gwp[at, lo] = lax.dot_general(
                mg[at, :], xf[lo, :], (((1,), (1,)), ((), ())), preferred_element_type=f32)
            return carry

        lax.fori_loop(0, 2, part, 0)

    top, bot = (0, 448), (448, 416)

    def gpart(d, half):
        return (pl.ds(*half), wcols(r + d))

    def pack(v, dst):
        n = v.shape[0]
        hi = v.astype(bf16)
        h = hi.astype(f32)
        big = jnp.abs(h) > 1e-34
        t = (v - h) / jnp.where(big, h, 1.0)
        lev = jnp.floor(t * 2560.0 + 0.5)
        dst[0:n] = hi
        dst[n:n + n // 2] = (lev[:n // 2] * 21.0 + lev[n // 2:]).astype(bf16)

    def unpack(src, n):
        h = src[0:n].astype(f32)
        both = src[n:n + n // 2].astype(f32)
        first = jnp.floor((both + 10.5) * (1.0 / 21.0))
        lev = jnp.concatenate([first, both - 21.0 * first], axis=0)
        return h + h * (lev * (1.0 / 2560.0))

    sent_u, sent_d = [], []

    def gw_send(direction, d, half, v=None):
        sent = sent_u if direction > 0 else sent_d
        side, i, n = (1 - direction) // 2, len(sent), half[1]
        pack(gwp[gpart(d, half)] if v is None else v, sg.at[side, i])
        sent.append(send(sg.at[side, i, 0:n + n // 2], rg.at[side, i, 0:n + n // 2],
                         up if direction > 0 else down))

    def gw_step(i):
        for direction, sent in ((1, sent_u), (-1, sent_d)):
            first, second = (top, bot) if direction > 0 else (bot, top)
            half = first if i % 2 == 0 else second
            d = direction * (3 - (i + 1) // 2)
            sent[i].wait_recv()
            at = gpart(d, half)
            v = gwp[at] + unpack(rg.at[(1 - direction) // 2, i], half[1])
            if d != 0:
                gw_send(direction, d, half, v)
            else:
                gwp[at] = v

    gw_tile(half_r + 2)
    gw_send(1, 4, top)
    gw_send(-1, -4, bot)
    forward_w(3, 1)
    gw_tile(half_r + 2 - sign)
    gw_send(1, 3, bot)
    gw_send(-1, -3, top)
    gi_turn(half_r - sign)
    gi_pair(half_r - sign, 0, 4)
    gi_turn(half_r + sign)
    gi_pair(half_r + sign, 0, 4)
    forward_w(4, 0)
    gi_turn(half_r + 2)

    mine, other = k * 512, (1 - k) * 512

    def gi_slice(l):
        gi_pair(half_r + 2, l, 1)
        return send(gip.at[l, rows(other, 512, 512)], r0.at[l], twin)

    def pass_one(l, base, unit, pos, right, left, buf):
        half = unit // 2

        def part(d, which):
            return (l, rows(base + lax.rem(pos + d + 8, 4) * unit + which * half, half, half))

        def go(i, d, which, peer):
            return send(gip.at[part(d, which)], buf.at[l, i], peer)

        first = [go(0, 2, 0, right), go(1, 2, 1, left), go(2, 1, 1, right), go(3, -1, 0, left)]

        def second():
            first[0].wait_recv()
            here = part(1, 0)
            gip[here] = gip[here] + buf[l, 0]
            first.append(go(4, 1, 0, right))
            first[1].wait_recv()
            here = part(-1, 1)
            gip[here] = gip[here] + buf[l, 1]
            first.append(go(5, -1, 1, left))

        def third():
            first[2].wait_recv()
            first[5].wait_recv()
            here = part(0, 1)
            gip[here] = gip[here] + (buf[l, 2] + buf[l, 5])
            first[3].wait_recv()
            first[4].wait_recv()
            here = part(0, 0)
            gip[here] = gip[here] + (buf[l, 3] + buf[l, 4])

        return second, third

    pair, stage_a, stage_b = {}, {}, {}

    def join(l):
        pair[l].wait_recv()
        here = (l, rows(mine, 512, 512))
        gip[here] = gip[here] + r0[l]
        stage_a[l] = pass_one(l, mine, 128, p, right_a, left_a, ra)

    def step_b(l):
        stage_a[l][1]()
        stage_b[l] = pass_one(l, mine + p * 128, 32, q, right_b, left_b, rb)

    def y_tile(n, carry):
        lo = rows(n * 512, 512, 512)
        for m in range(2):
            yv[m * 432:(m + 1) * 432, lo] = jnp.dot(
                wf[m * 432:(m + 1) * 432, :], xf[:, lo], preferred_element_type=f32)
        return carry


    def ys(lo, hi):
        lax.fori_loop(lo, hi, y_tile, 0)

    def plane(z):
        acc = None
        for j, (b, e) in enumerate(SHIFTS):
            t = None
            for a in (-1, 0, 1):
                if z + a in (0, 1):
                    lo = (a + 1) * 288 + j * 32
                    u = yv[lo:lo + 32, (z + a) * N:(z + a + 1) * N]
                    t = u if t is None else t + u
            s = (-(b * BX + e)) % N
            if s:
                t = jnp.where(valid(b, e), pltpu.roll(t, s, 1), 0.0)
            acc = t if acc is None else acc + t
        return acc

    def step_a2(l):
        stage_a[l][0]()

    def step_b2(l):
        stage_b[l][0]()

    def finish(l):
        stage_b[l][1]()

    own, edges = {}, {}

    def step_s(l):
        pair[l] = gi_slice(l)

    def step_t(i):
        gw_tile(half_r + 2 + (0, -sign, sign, 2)[i])

    def step_y(n):
        ys(n, n + 1)

    def step_p(z):
        if z in (0, 1):
            own[z] = plane(z)
        else:
            i = (z + 1) // 3
            edge_s[i] = plane(z)
            edges[i] = send(edge_s.at[i], edge_r.at[i], up if i else down)

    def step_o(z):
        edges[1 - z].wait_recv()
        gone = r == (NZ - 1 if z else 0)
        out_ref[z] = (own[z] + jnp.where(gone, 0.0, edge_r[1 - z])).astype(bf16)

    ops = dict(s=step_s, t=step_t, y=step_y, p=step_p, o=step_o, g=gw_step, j=join,
               a=step_a2, b=step_b, c=step_b2, f=finish)
    for word in SCHED:
        ops[word[0]](int(word[1:]))
    for l in range(SLICES):
        gi_ref[:, l * SL:(l + 1) * SL] = gip[l, rows(mine + p * 128 + q * 32, 32, 32), :].astype(bf16)
    gw_ref[...] = gwp[:, wcols(r)] * (1.0 / math.sqrt(16 * N))
    for copy in made:
        copy.wait_send()


def on_device(inputs, weight, grad_out):
    xr = inputs.transpose(1, 0, 2)
    wr = weight.transpose(1, 0, 2).reshape(27 * 32, 128)
    gr = grad_out.transpose(1, 0, 2)
    vm = pl.BlockSpec(memory_space=pltpu.VMEM)
    out, gi, gw = pl.pallas_call(
        kernel,
        out_shape=(jax.ShapeDtypeStruct((2, 32, N), bf16),
                   jax.ShapeDtypeStruct((32, 2 * N), bf16),
                   jax.ShapeDtypeStruct((864, 128), f32)),
        in_specs=[vm] * 3,
        out_specs=(vm,) * 3,
        scratch_shapes=[
            pltpu.VMEM((1024, 2 * N), bf16),
            pltpu.VMEM((864, 1024), bf16),
            pltpu.VMEM((256, 896), bf16),
            pltpu.VMEM((864, 2 * N), bf16),
            pltpu.VMEM((SLICES, 1024, SL), f32),
            pltpu.VMEM((864, 1024), f32),
            pltpu.VMEM((864, 2 * N), f32),
            pltpu.VMEM((2, 32, N), bf16),
            pltpu.VMEM((SLICES, 512, SL), f32),
            pltpu.VMEM((SLICES, 6, 64, SL), f32),
            pltpu.VMEM((SLICES, 6, 16, SL), f32),
            pltpu.VMEM((2, 7, 672, 128), bf16),
            pltpu.VMEM((2, 7, 672, 128), bf16),
            pltpu.VMEM((2, 32, N), f32),
            pltpu.VMEM((2, 32, N), f32),
            pltpu.SemaphoreType.DMA((NMSG,)),
            pltpu.SemaphoreType.DMA((NMSG,)),
        ],
        compiler_params=pltpu.CompilerParams(
            collective_id=0, has_side_effects=True, vmem_limit_bytes=58 << 20),
        name="layer",
    )(xr, wr, gr)
    return (out.transpose(1, 0, 2), gi.reshape(32, 2, N),
            gw.reshape(27, 32, 128).transpose(1, 0, 2))


def solution(mesh):
    placed = (P("col", "row", None), P("col", None, "row"), P("col", "row", None))
    return jax.shard_map(on_device, mesh=mesh, in_specs=placed, out_specs=placed[:1] * 2 + placed[1:2], check_vma=False)
```

```python
import math

import jax
import jax.numpy as jnp
from jax import lax
from jax.experimental import pallas as pl
from jax.experimental.pallas import tpu as pltpu
from jax.sharding import PartitionSpec as P

BX = 32
BY = 32
N = BX * BY
MESH = pl.DeviceIdType.MESH
f32 = jnp.float32
bf16 = jnp.bfloat16
SHIFTS = [(b, e) for b in (-1, 0, 1) for e in (-1, 0, 1)]
NX, NY, NZ = 4, 4, 8
SLICES = 4
SL = 2048 // SLICES
NMSG = 208
SCHED = (
    "s0", "s1", "s2", "g0", "j0", "t2", "s3", "j1", "g1", "a0", "y0", "t3", "j2", "a1",
    "b0", "g2", "y1", "y2", "j3", "a2", "b1", "c0", "g3", "y3", "p-1", "a3", "b2", "c1",
    "f0", "g4", "p2", "b3", "c2", "f1", "p0", "c3", "f2", "g5", "p1", "f3", "o0", "o1",
    "g6",
)


def valid(dy, dx):
    lane = lax.broadcasted_iota(jnp.int32, (1, N), 1)
    y = lane // BX + dy
    x = lane % BX + dx
    return (y >= 0) & (y < BY) & (x >= 0) & (x < BX)


def kernel(x_in, w_in, g_in, out_ref, gi_ref, gw_ref,
           xf, wf, wt, mg, gip, gwp, yv, halo, r0, ra, rb, rg, sg, edge_s, edge_r, ssem, rsem):
    r = lax.axis_index("row")
    c = lax.axis_index("col")
    x, y, k = c // 8, (c // 2) % 4, c % 2
    p = x * (1 - k) + y * k
    q = y * (1 - k) + x * k
    sa, sb = 8 - 6 * k, 2 + 6 * k

    def col(pp, qq):
        return lax.rem(pp + 8, 4) * sa + lax.rem(qq + 8, 4) * sb + k

    right_a, left_a = (r, col(p + 1, q)), (r, col(p - 1, q))
    right_b, left_b = (r, col(p, q + 1)), (r, col(p, q - 1))
    up, down = (lax.rem(r + 1, NZ), c), (lax.rem(r + 7, NZ), c)
    twin = (r, c + 1 - 2 * k)

    barrier = pltpu.get_barrier_semaphore()
    for peer in (right_a, left_a, right_b, left_b, up, down, twin):
        pl.semaphore_signal(barrier, inc=1, device_id=peer, device_id_type=MESH)
    pl.semaphore_wait(barrier, 7)

    made = []

    def send(src, dst, peer):
        i = len(made)
        copy = pltpu.make_async_remote_copy(
            src_ref=src, dst_ref=dst, send_sem=ssem.at[i], recv_sem=rsem.at[i],
            device_id=peer, device_id_type=MESH)
        copy.start()
        made.append(copy)
        return copy

    def rows(base, size, unit):
        return pl.ds(pl.multiple_of(base, unit), size)

    def block(pp, qq):
        return xf.at[rows(col(pp, qq) * 32, 32, 32)]

    def unit(pp, qq, h):
        return xf.at[rows(col(pp, qq) * 32 + 16 * h, 16, 16)]

    def wcols(rr):
        return rows(lax.rem(rr + 16, NZ) * 128, 128, 128)

    ar, al, fa = {}, {}, {}
    br, bl, fb = {}, {}, {}
    tw = []
    h_up = send(g_in.at[1], halo.at[0], up)
    h_dn = send(g_in.at[0], halo.at[1], down)
    for z in (0, 1):
        xf[rows(c * 32, 32, 32), z * N:(z + 1) * N] = x_in[z]
    for h in (0, 1):
        src, other_src = unit(p, q, h), unit(p, q, 1 - h)
        ar[h] = send(src, src, right_a)
        al[1 - h] = send(other_src, other_src, left_a)
        br[0, h] = send(src, src, right_b)
        bl[0, 1 - h] = send(other_src, other_src, left_b)
    wu, wd = {}, {}
    for i in (0, 1):
        for step, got, peer in ((i, wu, up), (1 - i, wd, down)):
            got[0, step] = send(w_in.at[432 * step:432 * step + 432],
                                wf.at[432 * step:432 * step + 432, wcols(r)], peer)
    tw.append(send(block(p, q), block(p, q), twin))
    wf[:, wcols(r)] = w_in[...]

    def build(src, plane):
        for j, (b, e) in enumerate(SHIFTS):
            s = (b * BX + e) % N
            v = src
            if s:
                v = jnp.where(valid(-b, -e), pltpu.roll(src, s, 1), 0.0)
            v = v.astype(bf16)
            for a in (-1, 0, 1):
                if plane + a in (0, 1):
                    lo = (a + 1) * 288 + j * 32
                    mg[lo:lo + 32, (plane + a) * N:(plane + a + 1) * N] = v

    def gi_turn(j):
        blk = wf[:, rows(lax.rem(j + 8, 4) * 256, 256, 256)].T
        for i in range(8):
            to = (i % 2) * 128 + (i // 2) * 32
            wt[to:to + 32, 0:864] = blk[i * 32:(i + 1) * 32]

    def gi_pair(j, start, tiles):
        jj = lax.rem(j + 8, 4)

        def tile(n, carry):
            o = jnp.dot(wt[:, 0:864], mg[:, rows(n * SL, SL, SL)], preferred_element_type=f32)
            gip[n, rows(jj * 128, 128, 128), :] = o[0:128]
            for i in range(4):
                gip[n, rows(512 + i * 128 + jj * 32, 32, 32), :] = o[128 + i * 32:160 + i * 32]
            return carry

        lax.fori_loop(start, start + tiles, tile, 0)

    half_r = r // 2
    sign = 1 - 2 * lax.rem(r, 2)

    def spread_b(d, h):
        u = unit(p + d, q, h)
        if h == 0:
            br[d, h] = send(u, u, right_b)
            bl[d, h] = send(u, u, left_b)
        else:
            bl[d, h] = send(u, u, left_b)
            br[d, h] = send(u, u, right_b)

    def share(pp, qq):
        tw.append(send(block(pp, qq), block(pp, qq), twin))

    def take_a(d, h):
        (ar if d < 0 else al)[h].wait_recv()
        u = unit(p + d, q, h)
        if (d, h) == (-1, 0):
            fa[0] = send(u, u, right_a)
        if (d, h) == (1, 1):
            fa[1] = send(u, u, left_a)
        spread_b(d, h)

    def take_b(d):
        br[d, 0].wait_recv()
        u = unit(p + d, q - 1, 0)
        fb[d, 0] = send(u, u, right_b)
        bl[d, 1].wait_recv()
        u = unit(p + d, q + 1, 1)
        fb[d, 1] = send(u, u, left_b)

    def rest_b(d):
        br[d, 1].wait_recv()
        share(p + d, q - 1)
        bl[d, 0].wait_recv()
        share(p + d, q + 1)

    def finish_b(d):
        fb[d, 0].wait_recv()
        fb[d, 1].wait_recv()
        share(p + d, q + 2)

    def forward_w(step, i):
        for got, peer, part, d in ((wu, up, i, -step), (wd, down, 1 - i, step)):
            got[step - 1, part].wait_recv()
            if step < 3 or (step == 3 and i == 0):
                here = wf.at[432 * part:432 * part + 432, wcols(r + d)]
                got[step, part] = send(here, here, peer)

    build(g_in[0].astype(f32), 0)
    take_a(-1, 0)
    take_a(1, 1)
    take_b(0)
    forward_w(1, 0)
    take_a(-1, 1)
    share(p - 1, q)
    take_a(1, 0)
    share(p + 1, q)
    for h in (0, 1):
        fa[h].wait_recv()
        spread_b(2, h)
    share(p + 2, q)
    rest_b(0)
    build(g_in[1].astype(f32), 1)
    take_b(-1)
    take_b(1)
    forward_w(1, 1)
    h_up.wait_recv()
    build(jnp.where(r == 0, 0.0, halo[0].astype(f32)), -1)
    finish_b(0)
    rest_b(-1)
    rest_b(1)
    forward_w(2, 0)
    h_dn.wait_recv()
    build(jnp.where(r == NZ - 1, 0.0, halo[1].astype(f32)), 2)
    take_b(2)
    gi_turn(half_r)
    forward_w(2, 1)
    finish_b(-1)
    finish_b(1)
    rest_b(2)
    gi_pair(half_r, 0, 2)
    forward_w(3, 0)
    finish_b(2)
    gi_pair(half_r, 2, 2)
    for copy in tw:
        copy.wait_recv()

    def gw_tile(j):
        lo = rows(lax.rem(j + 8, 4) * 256, 256, 256)

        def part(m, carry):
            at = rows(m * 432, 432, 16)
            gwp[at, lo] = lax.dot_general(
                mg[at, :], xf[lo, :], (((1,), (1,)), ((), ())), preferred_element_type=f32)
            return carry

        lax.fori_loop(0, 2, part, 0)

    top, bot = (0, 448), (448, 416)

    def gpart(d, half):
        return (pl.ds(*half), wcols(r + d))

    def pack(v, dst):
        n = v.shape[0]
        hi = v.astype(bf16)
        h = hi.astype(f32)
        big = jnp.abs(h) > 1e-34
        t = (v - h) / jnp.where(big, h, 1.0)
        lev = jnp.floor(t * 2560.0 + 0.5)
        dst[0:n] = hi
        dst[n:n + n // 2] = (lev[:n // 2] * 21.0 + lev[n // 2:]).astype(bf16)

    def unpack(src, n):
        h = src[0:n].astype(f32)
        both = src[n:n + n // 2].astype(f32)
        first = jnp.floor((both + 10.5) * (1.0 / 21.0))
        lev = jnp.concatenate([first, both - 21.0 * first], axis=0)
        return h + h * (lev * (1.0 / 2560.0))

    sent_u, sent_d = [], []

    def gw_send(direction, d, half, v=None):
        sent = sent_u if direction > 0 else sent_d
        side, i, n = (1 - direction) // 2, len(sent), half[1]
        pack(gwp[gpart(d, half)] if v is None else v, sg.at[side, i])
        sent.append(send(sg.at[side, i, 0:n + n // 2], rg.at[side, i, 0:n + n // 2],
                         up if direction > 0 else down))

    def gw_step(i):
        for direction, sent in ((1, sent_u), (-1, sent_d)):
            first, second = (top, bot) if direction > 0 else (bot, top)
            half = first if i % 2 == 0 else second
            d = direction * (3 - (i + 1) // 2)
            sent[i].wait_recv()
            at = gpart(d, half)
            v = gwp[at] + unpack(rg.at[(1 - direction) // 2, i], half[1])
            if d != 0:
                gw_send(direction, d, half, v)
            else:
                gwp[at] = v

    gw_tile(half_r + 2)
    gw_send(1, 4, top)
    gw_send(-1, -4, bot)
    forward_w(3, 1)
    gw_tile(half_r + 2 - sign)
    gw_send(1, 3, bot)
    gw_send(-1, -3, top)
    gi_turn(half_r - sign)
    gi_pair(half_r - sign, 0, 4)
    gi_turn(half_r + sign)
    gi_pair(half_r + sign, 0, 4)
    forward_w(4, 0)
    gi_turn(half_r + 2)

    mine, other = k * 512, (1 - k) * 512

    def gi_slice(l):
        gi_pair(half_r + 2, l, 1)
        return send(gip.at[l, rows(other, 512, 512)], r0.at[l], twin)

    def pass_one(l, base, unit, pos, right, left, buf):
        half = unit // 2

        def part(d, which):
            return (l, rows(base + lax.rem(pos + d + 8, 4) * unit + which * half, half, half))

        def go(i, d, which, peer):
            return send(gip.at[part(d, which)], buf.at[l, i], peer)

        first = [go(0, 2, 0, right), go(1, 2, 1, left), go(2, 1, 1, right), go(3, -1, 0, left)]

        def second():
            first[0].wait_recv()
            here = part(1, 0)
            gip[here] = gip[here] + buf[l, 0]
            first.append(go(4, 1, 0, right))
            first[1].wait_recv()
            here = part(-1, 1)
            gip[here] = gip[here] + buf[l, 1]
            first.append(go(5, -1, 1, left))

        def third():
            first[2].wait_recv()
            first[5].wait_recv()
            here = part(0, 1)
            gip[here] = gip[here] + (buf[l, 2] + buf[l, 5])
            first[3].wait_recv()
            first[4].wait_recv()
            here = part(0, 0)
            gip[here] = gip[here] + (buf[l, 3] + buf[l, 4])

        return second, third

    pair, stage_a, stage_b = {}, {}, {}

    def join(l):
        pair[l].wait_recv()
        here = (l, rows(mine, 512, 512))
        gip[here] = gip[here] + r0[l]
        stage_a[l] = pass_one(l, mine, 128, p, right_a, left_a, ra)

    def step_b(l):
        stage_a[l][1]()
        stage_b[l] = pass_one(l, mine + p * 128, 32, q, right_b, left_b, rb)

    def y_tile(n, carry):
        lo = rows(n * 512, 512, 512)
        for m in range(2):
            yv[m * 432:(m + 1) * 432, lo] = jnp.dot(
                wf[m * 432:(m + 1) * 432, :], xf[:, lo], preferred_element_type=f32)
        return carry


    def ys(lo, hi):
        lax.fori_loop(lo, hi, y_tile, 0)

    def plane(z):
        acc = None
        for j, (b, e) in enumerate(SHIFTS):
            t = None
            for a in (-1, 0, 1):
                if z + a in (0, 1):
                    lo = (a + 1) * 288 + j * 32
                    u = yv[lo:lo + 32, (z + a) * N:(z + a + 1) * N]
                    t = u if t is None else t + u
            s = (-(b * BX + e)) % N
            if s:
                t = jnp.where(valid(b, e), pltpu.roll(t, s, 1), 0.0)
            acc = t if acc is None else acc + t
        return acc

    def step_a2(l):
        stage_a[l][0]()

    def step_b2(l):
        stage_b[l][0]()

    def finish(l):
        stage_b[l][1]()

    own, edges = {}, {}

    def step_s(l):
        pair[l] = gi_slice(l)

    def step_t(i):
        gw_tile(half_r + 2 + (0, -sign, sign, 2)[i])

    def step_y(n):
        ys(n, n + 1)

    def step_p(z):
        if z in (0, 1):
            own[z] = plane(z)
        else:
            i = (z + 1) // 3
            edge_s[i] = plane(z)
            edges[i] = send(edge_s.at[i], edge_r.at[i], up if i else down)

    def step_o(z):
        edges[1 - z].wait_recv()
        gone = r == (NZ - 1 if z else 0)
        out_ref[z] = (own[z] + jnp.where(gone, 0.0, edge_r[1 - z])).astype(bf16)

    ops = dict(s=step_s, t=step_t, y=step_y, p=step_p, o=step_o, g=gw_step, j=join,
               a=step_a2, b=step_b, c=step_b2, f=finish)
    for word in SCHED:
        ops[word[0]](int(word[1:]))
    for l in range(SLICES):
        gi_ref[l * SL // N, :, l * SL % N:l * SL % N + SL] = gip[l, rows(mine + p * 128 + q * 32, 32, 32), :].astype(bf16)
    gw_ref[...] = gwp[:, wcols(r)] * (1.0 / math.sqrt(16 * N))
    for copy in made:
        copy.wait_send()


def on_device(inputs, weight, grad_out):
    xr = inputs.transpose(1, 0, 2)
    wr = weight.transpose(1, 0, 2).reshape(27 * 32, 128)
    gr = grad_out.transpose(1, 0, 2)
    vm = pl.BlockSpec(memory_space=pltpu.VMEM)
    out, gi, gw = pl.pallas_call(
        kernel,
        out_shape=(jax.ShapeDtypeStruct((2, 32, N), bf16),
                   jax.ShapeDtypeStruct((2, 32, N), bf16),
                   jax.ShapeDtypeStruct((864, 128), f32)),
        in_specs=[vm] * 3,
        out_specs=(vm,) * 3,
        scratch_shapes=[
            pltpu.VMEM((1024, 2 * N), bf16),
            pltpu.VMEM((864, 1024), bf16),
            pltpu.VMEM((256, 896), bf16),
            pltpu.VMEM((864, 2 * N), bf16),
            pltpu.VMEM((SLICES, 1024, SL), f32),
            pltpu.VMEM((864, 1024), f32),
            pltpu.VMEM((864, 2 * N), f32),
            pltpu.VMEM((2, 32, N), bf16),
            pltpu.VMEM((SLICES, 512, SL), f32),
            pltpu.VMEM((SLICES, 6, 64, SL), f32),
            pltpu.VMEM((SLICES, 6, 16, SL), f32),
            pltpu.VMEM((2, 7, 672, 128), bf16),
            pltpu.VMEM((2, 7, 672, 128), bf16),
            pltpu.VMEM((2, 32, N), f32),
            pltpu.VMEM((2, 32, N), f32),
            pltpu.SemaphoreType.DMA((NMSG,)),
            pltpu.SemaphoreType.DMA((NMSG,)),
        ],
        compiler_params=pltpu.CompilerParams(
            collective_id=0, has_side_effects=True, vmem_limit_bytes=58 << 20),
        name="layer",
    )(xr, wr, gr)
    return (out.transpose(1, 0, 2), gi.transpose(1, 0, 2),
            gw.reshape(27, 32, 128).transpose(1, 0, 2))


def solution(mesh):
    placed = (P("col", "row", None), P("col", None, "row"), P("col", "row", None))
    return jax.shard_map(on_device, mesh=mesh, in_specs=placed, out_specs=placed[:1] * 2 + placed[1:2], check_vma=False)
```

```python
import math

import jax
import jax.numpy as jnp
from jax import lax
from jax.experimental import pallas as pl
from jax.experimental.pallas import tpu as pltpu
from jax.sharding import PartitionSpec as P

BX = 32
BY = 32
N = BX * BY
MESH = pl.DeviceIdType.MESH
f32 = jnp.float32
bf16 = jnp.bfloat16
SHIFTS = [(b, e) for b in (-1, 0, 1) for e in (-1, 0, 1)]
NX, NY, NZ = 4, 4, 8
SLICES = 4
SL = 2048 // SLICES
NMSG = 208
SCHED = (
    "s0", "s1", "s2", "g0", "j0", "t2", "s3", "j1", "g1", "a0", "y0", "t3", "j2", "a1",
    "b0", "g2", "y1", "y2", "j3", "a2", "b1", "c0", "g3", "y3", "p-1", "a3", "b2", "c1",
    "f0", "g4", "p2", "b3", "c2", "f1", "p0", "c3", "f2", "g5", "p1", "f3", "o0", "o1",
    "g6",
)


def valid(dy, dx):
    lane = lax.broadcasted_iota(jnp.int32, (1, N), 1)
    y = lane // BX + dy
    x = lane % BX + dx
    return (y >= 0) & (y < BY) & (x >= 0) & (x < BX)


def kernel(x_in, w_in, g_in, out_ref, gw_ref,
           xf, wf, wt, mg, gip, gwp, yv, halo, r0, ra, rb, rg, sg, edge_s, edge_r, ssem, rsem):
    r = lax.axis_index("row")
    c = lax.axis_index("col")
    x, y, k = c // 8, (c // 2) % 4, c % 2
    p = x * (1 - k) + y * k
    q = y * (1 - k) + x * k
    sa, sb = 8 - 6 * k, 2 + 6 * k

    def col(pp, qq):
        return lax.rem(pp + 8, 4) * sa + lax.rem(qq + 8, 4) * sb + k

    right_a, left_a = (r, col(p + 1, q)), (r, col(p - 1, q))
    right_b, left_b = (r, col(p, q + 1)), (r, col(p, q - 1))
    up, down = (lax.rem(r + 1, NZ), c), (lax.rem(r + 7, NZ), c)
    twin = (r, c + 1 - 2 * k)

    barrier = pltpu.get_barrier_semaphore()
    for peer in (right_a, left_a, right_b, left_b, up, down, twin):
        pl.semaphore_signal(barrier, inc=1, device_id=peer, device_id_type=MESH)
    pl.semaphore_wait(barrier, 7)

    made = []

    def send(src, dst, peer):
        i = len(made)
        copy = pltpu.make_async_remote_copy(
            src_ref=src, dst_ref=dst, send_sem=ssem.at[i], recv_sem=rsem.at[i],
            device_id=peer, device_id_type=MESH)
        copy.start()
        made.append(copy)
        return copy

    def rows(base, size, unit):
        return pl.ds(pl.multiple_of(base, unit), size)

    def block(pp, qq):
        return xf.at[rows(col(pp, qq) * 32, 32, 32)]

    def unit(pp, qq, h):
        return xf.at[rows(col(pp, qq) * 32 + 16 * h, 16, 16)]

    def wcols(rr):
        return rows(lax.rem(rr + 16, NZ) * 128, 128, 128)

    ar, al, fa = {}, {}, {}
    br, bl, fb = {}, {}, {}
    tw = []
    h_up = send(g_in.at[1], halo.at[0], up)
    h_dn = send(g_in.at[0], halo.at[1], down)
    for z in (0, 1):
        xf[rows(c * 32, 32, 32), z * N:(z + 1) * N] = x_in[z]
    for h in (0, 1):
        src, other_src = unit(p, q, h), unit(p, q, 1 - h)
        ar[h] = send(src, src, right_a)
        al[1 - h] = send(other_src, other_src, left_a)
        br[0, h] = send(src, src, right_b)
        bl[0, 1 - h] = send(other_src, other_src, left_b)
    wu, wd = {}, {}
    for i in (0, 1):
        for step, got, peer in ((i, wu, up), (1 - i, wd, down)):
            got[0, step] = send(w_in.at[432 * step:432 * step + 432],
                                wf.at[432 * step:432 * step + 432, wcols(r)], peer)
    tw.append(send(block(p, q), block(p, q), twin))
    wf[:, wcols(r)] = w_in[...]

    def build(src, plane):
        for j, (b, e) in enumerate(SHIFTS):
            s = (b * BX + e) % N
            v = src
            if s:
                v = jnp.where(valid(-b, -e), pltpu.roll(src, s, 1), 0.0)
            v = v.astype(bf16)
            for a in (-1, 0, 1):
                if plane + a in (0, 1):
                    lo = (a + 1) * 288 + j * 32
                    mg[lo:lo + 32, (plane + a) * N:(plane + a + 1) * N] = v

    def gi_turn(j):
        blk = wf[:, rows(lax.rem(j + 8, 4) * 256, 256, 256)].T
        for i in range(8):
            to = (i % 2) * 128 + (i // 2) * 32
            wt[to:to + 32, 0:864] = blk[i * 32:(i + 1) * 32]

    def gi_pair(j, start, tiles):
        jj = lax.rem(j + 8, 4)

        def tile(n, carry):
            o = jnp.dot(wt[:, 0:864], mg[:, rows(n * SL, SL, SL)], preferred_element_type=f32)
            gip[n, rows(jj * 128, 128, 128), :] = o[0:128]
            for i in range(4):
                gip[n, rows(512 + i * 128 + jj * 32, 32, 32), :] = o[128 + i * 32:160 + i * 32]
            return carry

        lax.fori_loop(start, start + tiles, tile, 0)

    half_r = r // 2
    sign = 1 - 2 * lax.rem(r, 2)

    def spread_b(d, h):
        u = unit(p + d, q, h)
        if h == 0:
            br[d, h] = send(u, u, right_b)
            bl[d, h] = send(u, u, left_b)
        else:
            bl[d, h] = send(u, u, left_b)
            br[d, h] = send(u, u, right_b)

    def share(pp, qq):
        tw.append(send(block(pp, qq), block(pp, qq), twin))

    def take_a(d, h):
        (ar if d < 0 else al)[h].wait_recv()
        u = unit(p + d, q, h)
        if (d, h) == (-1, 0):
            fa[0] = send(u, u, right_a)
        if (d, h) == (1, 1):
            fa[1] = send(u, u, left_a)
        spread_b(d, h)

    def take_b(d):
        br[d, 0].wait_recv()
        u = unit(p + d, q - 1, 0)
        fb[d, 0] = send(u, u, right_b)
        bl[d, 1].wait_recv()
        u = unit(p + d, q + 1, 1)
        fb[d, 1] = send(u, u, left_b)

    def rest_b(d):
        br[d, 1].wait_recv()
        share(p + d, q - 1)
        bl[d, 0].wait_recv()
        share(p + d, q + 1)

    def finish_b(d):
        fb[d, 0].wait_recv()
        fb[d, 1].wait_recv()
        share(p + d, q + 2)

    def forward_w(step, i):
        for got, peer, part, d in ((wu, up, i, -step), (wd, down, 1 - i, step)):
            got[step - 1, part].wait_recv()
            if step < 3 or (step == 3 and i == 0):
                here = wf.at[432 * part:432 * part + 432, wcols(r + d)]
                got[step, part] = send(here, here, peer)

    build(g_in[0].astype(f32), 0)
    take_a(-1, 0)
    take_a(1, 1)
    take_b(0)
    forward_w(1, 0)
    take_a(-1, 1)
    share(p - 1, q)
    take_a(1, 0)
    share(p + 1, q)
    for h in (0, 1):
        fa[h].wait_recv()
        spread_b(2, h)
    share(p + 2, q)
    rest_b(0)
    build(g_in[1].astype(f32), 1)
    take_b(-1)
    take_b(1)
    forward_w(1, 1)
    h_up.wait_recv()
    build(jnp.where(r == 0, 0.0, halo[0].astype(f32)), -1)
    finish_b(0)
    rest_b(-1)
    rest_b(1)
    forward_w(2, 0)
    h_dn.wait_recv()
    build(jnp.where(r == NZ - 1, 0.0, halo[1].astype(f32)), 2)
    take_b(2)
    gi_turn(half_r)
    forward_w(2, 1)
    finish_b(-1)
    finish_b(1)
    rest_b(2)
    gi_pair(half_r, 0, 2)
    forward_w(3, 0)
    finish_b(2)
    gi_pair(half_r, 2, 2)
    for copy in tw:
        copy.wait_recv()

    def gw_tile(j):
        lo = rows(lax.rem(j + 8, 4) * 256, 256, 256)

        def part(m, carry):
            at = rows(m * 432, 432, 16)
            gwp[at, lo] = lax.dot_general(
                mg[at, :], xf[lo, :], (((1,), (1,)), ((), ())), preferred_element_type=f32)
            return carry

        lax.fori_loop(0, 2, part, 0)

    top, bot = (0, 448), (448, 416)

    def gpart(d, half):
        return (pl.ds(*half), wcols(r + d))

    def pack(v, dst):
        n = v.shape[0]
        hi = v.astype(bf16)
        h = hi.astype(f32)
        big = jnp.abs(h) > 1e-34
        t = (v - h) / jnp.where(big, h, 1.0)
        lev = jnp.floor(t * 2560.0 + 0.5)
        dst[0:n] = hi
        dst[n:n + n // 2] = (lev[:n // 2] * 21.0 + lev[n // 2:]).astype(bf16)

    def unpack(src, n):
        h = src[0:n].astype(f32)
        both = src[n:n + n // 2].astype(f32)
        first = jnp.floor((both + 10.5) * (1.0 / 21.0))
        lev = jnp.concatenate([first, both - 21.0 * first], axis=0)
        return h + h * (lev * (1.0 / 2560.0))

    sent_u, sent_d = [], []

    def gw_send(direction, d, half, v=None):
        sent = sent_u if direction > 0 else sent_d
        side, i, n = (1 - direction) // 2, len(sent), half[1]
        pack(gwp[gpart(d, half)] if v is None else v, sg.at[side, i])
        sent.append(send(sg.at[side, i, 0:n + n // 2], rg.at[side, i, 0:n + n // 2],
                         up if direction > 0 else down))

    def gw_step(i):
        for direction, sent in ((1, sent_u), (-1, sent_d)):
            first, second = (top, bot) if direction > 0 else (bot, top)
            half = first if i % 2 == 0 else second
            d = direction * (3 - (i + 1) // 2)
            sent[i].wait_recv()
            at = gpart(d, half)
            v = gwp[at] + unpack(rg.at[(1 - direction) // 2, i], half[1])
            if d != 0:
                gw_send(direction, d, half, v)
            else:
                gwp[at] = v

    gw_tile(half_r + 2)
    gw_send(1, 4, top)
    gw_send(-1, -4, bot)
    forward_w(3, 1)
    gw_tile(half_r + 2 - sign)
    gw_send(1, 3, bot)
    gw_send(-1, -3, top)
    gi_turn(half_r - sign)
    gi_pair(half_r - sign, 0, 4)
    gi_turn(half_r + sign)
    gi_pair(half_r + sign, 0, 4)
    forward_w(4, 0)
    gi_turn(half_r + 2)

    mine, other = k * 512, (1 - k) * 512

    def gi_slice(l):
        gi_pair(half_r + 2, l, 1)
        return send(gip.at[l, rows(other, 512, 512)], r0.at[l], twin)

    def pass_one(l, base, unit, pos, right, left, buf):
        half = unit // 2

        def part(d, which):
            return (l, rows(base + lax.rem(pos + d + 8, 4) * unit + which * half, half, half))

        def go(i, d, which, peer):
            return send(gip.at[part(d, which)], buf.at[l, i], peer)

        first = [go(0, 2, 0, right), go(1, 2, 1, left), go(2, 1, 1, right), go(3, -1, 0, left)]

        def second():
            first[0].wait_recv()
            here = part(1, 0)
            gip[here] = gip[here] + buf[l, 0]
            first.append(go(4, 1, 0, right))
            first[1].wait_recv()
            here = part(-1, 1)
            gip[here] = gip[here] + buf[l, 1]
            first.append(go(5, -1, 1, left))

        def third():
            first[2].wait_recv()
            first[5].wait_recv()
            here = part(0, 1)
            gip[here] = gip[here] + (buf[l, 2] + buf[l, 5])
            first[3].wait_recv()
            first[4].wait_recv()
            here = part(0, 0)
            gip[here] = gip[here] + (buf[l, 3] + buf[l, 4])

        return second, third

    pair, stage_a, stage_b = {}, {}, {}

    def join(l):
        pair[l].wait_recv()
        here = (l, rows(mine, 512, 512))
        gip[here] = gip[here] + r0[l]
        stage_a[l] = pass_one(l, mine, 128, p, right_a, left_a, ra)

    def step_b(l):
        stage_a[l][1]()
        stage_b[l] = pass_one(l, mine + p * 128, 32, q, right_b, left_b, rb)

    def y_tile(n, carry):
        lo = rows(n * 512, 512, 512)
        for m in range(2):
            yv[m * 432:(m + 1) * 432, lo] = jnp.dot(
                wf[m * 432:(m + 1) * 432, :], xf[:, lo], preferred_element_type=f32)
        return carry


    def ys(lo, hi):
        lax.fori_loop(lo, hi, y_tile, 0)

    def plane(z):
        acc = None
        for j, (b, e) in enumerate(SHIFTS):
            t = None
            for a in (-1, 0, 1):
                if z + a in (0, 1):
                    lo = (a + 1) * 288 + j * 32
                    u = yv[lo:lo + 32, (z + a) * N:(z + a + 1) * N]
                    t = u if t is None else t + u
            s = (-(b * BX + e)) % N
            if s:
                t = jnp.where(valid(b, e), pltpu.roll(t, s, 1), 0.0)
            acc = t if acc is None else acc + t
        return acc

    def step_a2(l):
        stage_a[l][0]()

    def step_b2(l):
        stage_b[l][0]()

    def finish(l):
        stage_b[l][1]()

    own, edges = {}, {}

    def step_s(l):
        pair[l] = gi_slice(l)

    def step_t(i):
        gw_tile(half_r + 2 + (0, -sign, sign, 2)[i])

    def step_y(n):
        ys(n, n + 1)

    def step_p(z):
        if z in (0, 1):
            own[z] = plane(z)
        else:
            i = (z + 1) // 3
            edge_s[i] = plane(z)
            edges[i] = send(edge_s.at[i], edge_r.at[i], up if i else down)

    def step_o(z):
        edges[1 - z].wait_recv()
        gone = r == (NZ - 1 if z else 0)
        out_ref[z, 0:32] = (own[z] + jnp.where(gone, 0.0, edge_r[1 - z])).astype(bf16)

    ops = dict(s=step_s, t=step_t, y=step_y, p=step_p, o=step_o, g=gw_step, j=join,
               a=step_a2, b=step_b, c=step_b2, f=finish)
    for word in SCHED:
        ops[word[0]](int(word[1:]))
    for l in range(SLICES):
        out_ref[l * SL // N, 32:64, l * SL % N:l * SL % N + SL] = gip[l, rows(mine + p * 128 + q * 32, 32, 32), :].astype(bf16)
    gw_ref[...] = gwp[:, wcols(r)] * (1.0 / math.sqrt(16 * N))
    for copy in made:
        copy.wait_send()


def on_device(inputs, weight, grad_out):
    xr = inputs.transpose(1, 0, 2)
    wr = weight.transpose(1, 0, 2).reshape(27 * 32, 128)
    gr = grad_out.transpose(1, 0, 2)
    vm = pl.BlockSpec(memory_space=pltpu.VMEM)
    fields, gw = pl.pallas_call(
        kernel,
        out_shape=(jax.ShapeDtypeStruct((2, 64, N), bf16),
                   jax.ShapeDtypeStruct((864, 128), f32)),
        in_specs=[vm] * 3,
        out_specs=(vm,) * 2,
        scratch_shapes=[
            pltpu.VMEM((1024, 2 * N), bf16),
            pltpu.VMEM((864, 1024), bf16),
            pltpu.VMEM((256, 896), bf16),
            pltpu.VMEM((864, 2 * N), bf16),
            pltpu.VMEM((SLICES, 1024, SL), f32),
            pltpu.VMEM((864, 1024), f32),
            pltpu.VMEM((864, 2 * N), f32),
            pltpu.VMEM((2, 32, N), bf16),
            pltpu.VMEM((SLICES, 512, SL), f32),
            pltpu.VMEM((SLICES, 6, 64, SL), f32),
            pltpu.VMEM((SLICES, 6, 16, SL), f32),
            pltpu.VMEM((2, 7, 672, 128), bf16),
            pltpu.VMEM((2, 7, 672, 128), bf16),
            pltpu.VMEM((2, 32, N), f32),
            pltpu.VMEM((2, 32, N), f32),
            pltpu.SemaphoreType.DMA((NMSG,)),
            pltpu.SemaphoreType.DMA((NMSG,)),
        ],
        compiler_params=pltpu.CompilerParams(
            collective_id=0, has_side_effects=True, vmem_limit_bytes=58 << 20),
        name="layer",
    )(xr, wr, gr)
    fields = fields.transpose(1, 0, 2)
    return (fields[:32], fields[32:],
            gw.reshape(27, 32, 128).transpose(1, 0, 2))


def solution(mesh):
    placed = (P("col", "row", None), P("col", None, "row"), P("col", "row", None))
    return jax.shard_map(on_device, mesh=mesh, in_specs=placed, out_specs=placed[:1] * 2 + placed[1:2], check_vma=False)
```
